32 devices in a mesh: dp: 8 (over z, y), seq: 4 (over x, core).
Axes of the slice: x: 2, y: 2, z: 4, core: 2. Of those that a mesh axis runs over, the one named last changes fastest.
Arguments:
- hidden: bfloat16 [4096, 8192], P(('dp', 'seq')), may hold values from -24 to 24
- queries: bfloat16 [4096, 1024], P(('dp', 'seq')), may hold values from -32 to 32
- kv_weight: bfloat16 [8192, 256], P(('dp', 'seq')), may hold values from -1 to 1
- dest_device: int32 [4096], P(('dp', 'seq')), may hold values from 0 to 3, as said below
- segment_ids: int32 [8, 512], P('dp'), may hold values from 0 to 3, never falling along the last dimension, each value on 1 to 256 neighbouring positions
Outputs:
- attended: bfloat16 [4096, 1024], P(('dp', 'seq'))
The draws below stay inside these ranges and needn't reach their ends.
Inputs may be any that keep to these rules, and one draw needn't show every extreme that they name: `dest_device`: within a batch group, the number of tokens that device i of seq packs onto device j depends only on (j - i) mod 4; it is at most 32, exactly 32 for some pair of every group, and every device receives 128 tokens.
All inputs are finite; a program needn't handle non-finite values.
Results may differ from the reference program's by a relative error of at most 0.0058.
Values may be sent and summed in bfloat16 or wider, within the bound.
A program may use at most 64 MiB of HBM per device.

```python
import math
import jax
import jax.numpy as jnp
import numpy as np
from jax import lax

D = 8192
HEAD = 128
GROUP = 8
TOK_DEV = 128
MOST = 256
GROUP_ROWS = 512
ROWS = 4096
N_DP = 8
N_SEQ = 4


def shared_parts(key):
    matrix = jax.random.normal(jax.random.fold_in(key, 701), (D, 2 * HEAD), jnp.float32) / D ** 0.5
    matrix = jnp.clip(matrix, -6.0 / D ** 0.5, 6.0 / D ** 0.5)
    return matrix


def draw_kv_weight(key, part):
    matrix = shared_parts(key)
    return matrix.astype(jnp.bfloat16)


def draw_hidden(key, part):
    noise = jax.random.normal(jax.random.fold_in(key, 703), (ROWS, D), jnp.float32)
    values = jnp.clip(noise, -6.0, 6.0)
    return values.astype(jnp.bfloat16)


def draw_queries(key, part):
    noise = jax.random.normal(jax.random.fold_in(key, 705), (ROWS, GROUP * HEAD), jnp.float32)
    values = jnp.clip(noise, -6.0, 6.0)
    return values.astype(jnp.bfloat16)


def draw_dest_device(key, part):
    slots = TOK_DEV // 4

    def one_group(group_key):
        first_key, second_key, third_key = jax.random.split(group_key, 3)
        fullest = jax.random.randint(first_key, (), 0, N_SEQ)
        others = (fullest + 1 + jnp.arange((N_SEQ - 1) * slots) // slots) % N_SEQ
        others = jax.random.permutation(second_key, others)
        offsets = jnp.concatenate([jnp.full((slots,), fullest, jnp.int32), others[:TOK_DEV - slots].astype(jnp.int32)])

        def per_source(source, source_key):
            order = jax.random.permutation(source_key, TOK_DEV)
            return (source + offsets[order]) % N_SEQ
        table = jax.vmap(per_source)(jnp.arange(N_SEQ, dtype=jnp.int32), jax.random.split(third_key, N_SEQ))
        return table.reshape(N_SEQ * TOK_DEV)
    result = jax.vmap(one_group)(jax.random.split(key, N_DP))
    return result.reshape(ROWS).astype(jnp.int32)


def split_up(amount, total, limit, lean):
    loads = [(1 << 20) // math.isqrt(standing ** lean) + 1 for standing in range(2, amount + 1)]
    spare, holding = total - limit - (amount - 1), [1] * (amount - 1)
    while spare > 0:
        free = [i for i in range(amount - 1) if holding[i] < limit]
        mass, budget = sum([loads[i] for i in free]), spare
        for i in free:
            addition = min(limit - holding[i], max(1, budget * loads[i] // mass), spare)
            holding[i] = holding[i] + addition
            spare = spare - addition
    return np.array([limit] + holding)


def uneven_parts(own_key, amount, total, bound, lean):
    if amount == 2:
        one = jax.random.randint(own_key, (), max(1, total - bound), min(bound, total - 1) + 1)
        return jnp.stack([one, total - one])
    sizes = jnp.asarray(split_up(amount, total, bound, lean), jnp.int32)
    couples = (amount - 1) // 2
    donor, receiver = sizes[1:1 + 2 * couples:2], sizes[2:2 + 2 * couples:2]
    slack = jnp.minimum(donor - 1, bound - receiver)
    passed = jax.random.randint(jax.random.fold_in(own_key, 1), (couples,), 0, 1 << 20) % (slack + 1)
    sizes = sizes.at[1:1 + 2 * couples:2].set(donor - passed).at[2:2 + 2 * couples:2].set(receiver + passed)
    return sizes[jax.random.permutation(jax.random.fold_in(own_key, 2), amount)]


def setup_inputs(seed: int = 0) -> dict:
    streams_of = jax.random.split(jax.random.key(seed), 6)
    return {
        "hidden": draw_hidden(jax.random.fold_in(streams_of[5], 71), 0),
        "queries": draw_queries(jax.random.fold_in(streams_of[5], 71), 0),
        "kv_weight": draw_kv_weight(jax.random.fold_in(streams_of[5], 71), 0),
        "dest_device": draw_dest_device(jax.random.fold_in(streams_of[5], 71), 0),
        "segment_ids": jax.vmap(lambda own: jnp.searchsorted(jnp.cumsum(uneven_parts(own, 4, GROUP_ROWS, MOST, 1)), jnp.arange(GROUP_ROWS), side="right"))(jax.random.split(streams_of[4], N_DP)).reshape((N_DP, GROUP_ROWS)).astype(jnp.int32),
    }


def reference(hidden, queries, kv_weight, dest_device, segment_ids):
    rows_dev = TOK_DEV
    width_q = GROUP * HEAD
    reach = N_SEQ // 2
    padding = reach * rows_dev
    scale = 1.0 / (HEAD ** 0.5)

    def one_group(inputs):
        hid_group, qry_group, dest_group, segment = inputs
        kv_vals = jnp.dot(hid_group, kv_weight, preferred_element_type=jnp.float32).astype(jnp.bfloat16)
        feats = jnp.concatenate([qry_group, kv_vals], axis=1)
        order = jnp.argsort(dest_group, stable=True).astype(jnp.int32)
        packed = feats[order]
        keys_all = jnp.concatenate([jnp.zeros((padding, 2 * HEAD), jnp.bfloat16), packed[:, width_q:]], axis=0)
        seg_pad = jnp.concatenate([jnp.full((padding,), -1, jnp.int32), segment.astype(jnp.int32)])

        def block_out(block):
            start = (block * rows_dev).astype(jnp.int32)
            query_rows = lax.dynamic_slice_in_dim(packed, start, rows_dev, 0)[:, :width_q]
            query_rows = query_rows.reshape(rows_dev, GROUP, HEAD).astype(jnp.float32)
            window = lax.dynamic_slice_in_dim(keys_all, start, padding + rows_dev, 0)
            key_seg = lax.dynamic_slice_in_dim(seg_pad, start, padding + rows_dev, 0)
            query_seg = lax.dynamic_slice_in_dim(segment.astype(jnp.int32), start, rows_dev, 0)
            query_pos = start + jnp.arange(rows_dev, dtype=jnp.int32)
            key_pos = start - padding + jnp.arange(padding + rows_dev, dtype=jnp.int32)
            scores = jnp.einsum('rgh,kh->grk', query_rows, window[:, :HEAD].astype(jnp.float32)) * scale
            allow = (query_seg[:, None] == key_seg[None, :]) & (key_pos[None, :] <= query_pos[:, None])
            allow = allow[None, :, :]
            top = jnp.max(jnp.where(allow, scores, -jnp.inf), axis=-1, keepdims=True)
            weights = jnp.where(allow, jnp.exp(scores - top), 0.0)
            total = jnp.sum(weights, axis=-1)
            numer = jnp.einsum('grk,kh->grh', weights.astype(jnp.bfloat16).astype(jnp.float32), window[:, HEAD:].astype(jnp.float32))
            result = (numer / total[:, :, None]).astype(jnp.bfloat16)
            return jnp.transpose(result, (1, 0, 2)).reshape(rows_dev, width_q)

        blocks = lax.map(block_out, jnp.arange(N_SEQ, dtype=jnp.int32))
        return blocks.reshape(N_SEQ * rows_dev, width_q)

    hid_all = hidden.reshape(N_DP, GROUP_ROWS, D)
    qry_all = queries.reshape(N_DP, GROUP_ROWS, width_q)
    dest_all = dest_device.reshape(N_DP, GROUP_ROWS)
    result = lax.map(one_group, (hid_all, qry_all, dest_all, segment_ids))
    return result.reshape(ROWS, width_q)
```

```python
import functools

import jax
import jax.numpy as jnp
from jax import lax
from jax.experimental import pallas as pl
from jax.experimental.pallas import tpu as pltpu
from jax.sharding import PartitionSpec as P

HEAD = 128
GROUP = 8
PIECES = 1
MESH = pl.DeviceIdType.MESH


def shifted(shard, axis, by):
    devices = lax.axis_size(axis)
    pairs = [(i, i + by) for i in range(devices) if 0 <= i + by < devices]
    return lax.ppermute(shard, axis, pairs)


def shards(hidden, queries, kv_weight, dest_device, segment_ids):
    rows_dev = hidden.shape[0]
    width_q = GROUP * HEAD
    seq_count = lax.axis_size("seq")
    mine_index = lax.axis_index("seq")
    slots = rows_dev // 4
    reach = seq_count // 2
    scale = 1.0 / HEAD**0.5
    whole_weight = lax.all_gather(kv_weight, ("dp", "seq"), axis=0, tiled=True)
    kv_sum = jnp.dot(hidden, whole_weight, preferred_element_type=jnp.float32)
    kv_vals = kv_sum.astype(jnp.bfloat16)
    feats = jnp.concatenate([queries, kv_vals], axis=1)
    lanes = jnp.arange(seq_count, dtype=jnp.int32)
    offsets = (dest_device - mine_index) % seq_count
    member = (offsets[:, None] == lanes[None, :]).astype(jnp.int32)
    counts = jnp.sum(member, axis=0)
    dest_member = (dest_device[:, None] == lanes[None, :]).astype(jnp.int32)
    rank_in = jnp.sum((jnp.cumsum(dest_member, axis=0) - 1) * dest_member, axis=1)
    send_slot = dest_device * slots + rank_in
    select = (jnp.arange(seq_count * slots, dtype=jnp.int32)[:, None] == send_slot[None, :]).astype(
        jnp.bfloat16
    )
    outgoing = jnp.dot(select, feats, preferred_element_type=jnp.float32).astype(jnp.bfloat16)
    outgoing = outgoing.reshape(seq_count, slots, feats.shape[1])
    received = lax.all_to_all(outgoing, "seq", split_axis=0, concat_axis=0, tiled=True).reshape(
        seq_count * slots, feats.shape[1]
    )
    lookup = ((mine_index - lanes) % seq_count)[:, None] == lanes[None, :]
    from_count = jnp.sum(jnp.where(lookup, counts[None, :], 0), axis=1)
    from_start = jnp.cumsum(from_count) - from_count
    slot_index = jnp.broadcast_to(jnp.arange(slots, dtype=jnp.int32)[None, :], (seq_count, slots))
    dest_pos = (from_start[:, None] + slot_index).reshape(-1)
    valid = (slot_index < from_count[:, None]).reshape(-1)
    placer = (
        (jnp.arange(rows_dev, dtype=jnp.int32)[:, None] == dest_pos[None, :]) & valid[None, :]
    ).astype(jnp.bfloat16)
    packed = jnp.dot(placer, received, preferred_element_type=jnp.float32).astype(jnp.bfloat16)
    query_rows = packed[:, :width_q].reshape(rows_dev, GROUP, HEAD)
    kv_local = packed[:, width_q:]
    seg_row = segment_ids[0]
    own_start = mine_index * rows_dev
    query_seg = lax.dynamic_slice_in_dim(seg_row, own_start, rows_dev, 0)
    query_pos = own_start + jnp.arange(rows_dev, dtype=jnp.int32)

    def attend(carry, piece, start):
        top_old, total_old, numer_old = carry
        count_keys = piece.shape[0]
        key_pos = start + jnp.arange(count_keys, dtype=jnp.int32)
        key_seg = lax.dynamic_slice_in_dim(seg_row, jnp.maximum(start, 0), count_keys, 0)
        allow = (
            (query_seg[:, None] == key_seg[None, :])
            & (key_pos[None, :] <= query_pos[:, None])
            & (key_pos[None, :] >= 0)
        )
        allow = allow[None, :, :]
        scores = (
            jnp.einsum(
                "rgh,kh->grk", query_rows, piece[:, :HEAD], preferred_element_type=jnp.float32
            )
            * scale
        )
        top_new = jnp.maximum(top_old, jnp.max(jnp.where(allow, scores, -1e30), axis=-1))
        weights = jnp.where(allow, jnp.exp(scores - top_new[:, :, None]), 0.0)
        factor = jnp.exp(top_old - top_new)
        total_new = total_old * factor + jnp.sum(weights, axis=-1)
        contrib = jnp.einsum(
            "grk,kh->grh",
            weights.astype(jnp.bfloat16),
            piece[:, HEAD:],
            preferred_element_type=jnp.float32,
        )
        numer_new = numer_old * factor[:, :, None] + contrib
        return (top_new, total_new, numer_new)

    start_carry = (
        jnp.full((GROUP, rows_dev), -1e30, jnp.float32),
        jnp.zeros((GROUP, rows_dev), jnp.float32),
        jnp.zeros((GROUP, rows_dev, HEAD), jnp.float32),
    )
    state = attend(start_carry, kv_local, own_start)
    for back in range(1, reach + 1):
        earlier = shifted(kv_local, "seq", back)
        state = attend(state, earlier, own_start - back * rows_dev)
    top_val, total, numer = state
    result = (numer / total[:, :, None]).astype(jnp.bfloat16)
    return jnp.transpose(result, (1, 0, 2)).reshape(rows_dev, width_q)


def fused(
    nz, ny, nx, hid_hbm, qry_hbm, w_hbm, dest_ref, seg_ref, out_ref,
    hid, qry, wbuf, outgoing, received, dest_all, kv_all, packed, bias, acc,
    load_sem, w_send, w_recv, small_send, dest_recv, qry_recv, kv_recv,
):
    rows = hid.shape[0]
    depth = wbuf.shape[1]
    n_seq = nx * 2
    slots = rows // 4
    keys = n_seq * rows
    group = lax.axis_index("dp")
    me = lax.axis_index("seq")
    z, y = lax.div(group, ny), lax.rem(group, ny)
    x, c = lax.div(me, 2), lax.rem(me, 2)
    x1, y1 = x + (1 - c) * (1 - 2 * x), y + c * (1 - 2 * y)
    x3, y3 = x + c * (1 - 2 * x), y + (1 - c) * (1 - 2 * y)
    xo, yo = 1 - x, 1 - y

    def dev(zz, yy, xx, cc):
        return (zz * ny + yy, xx * 2 + cc)

    def block_of(zz, yy, xx, cc):
        return (zz * ny + yy) * n_seq + xx * 2 + cc

    first, third = dev(z, y1, x1, c), dev(z, y3, x3, c)
    partner = dev(z, y, x, 1 - c)
    peers = [lax.rem(me + i, n_seq) for i in range(1, n_seq)]

    mine = block_of(z, y, x, c)
    load_q = pltpu.make_async_copy(qry_hbm, qry, load_sem.at[0])
    load_w = pltpu.make_async_copy(w_hbm, wbuf.at[mine], load_sem.at[1])
    load_h = pltpu.make_async_copy(hid_hbm, hid, load_sem.at[2])
    load_q.start()
    load_w.start()
    load_h.start()

    barrier = pltpu.get_barrier_semaphore()
    for peer in peers:
        pl.semaphore_signal(barrier, inc=1, device_id=(group, peer), device_id_type=MESH)
    pl.semaphore_signal(barrier, inc=1, device_id=dev(z, yo, x, c), device_id_type=MESH)

    @pl.when(z > 0)
    def _():
        pl.semaphore_signal(barrier, inc=1, device_id=dev(z - 1, y, x, c), device_id_type=MESH)

    @pl.when(z < nz - 1)
    def _():
        pl.semaphore_signal(barrier, inc=1, device_id=dev(z + 1, y, x, c), device_id_type=MESH)

    above, below = (z < nz - 1).astype(jnp.int32), (z > 0).astype(jnp.int32)
    pl.semaphore_wait(barrier, n_seq + above + below)

    pending = []
    count = [0]

    def small(src, dst, recv, where, number):
        copy = pltpu.make_async_remote_copy(
            src_ref=src, dst_ref=dst, send_sem=small_send.at[number], recv_sem=recv,
            device_id=where, device_id_type=MESH,
        )
        copy.start()
        pending.append((None, copy))

    for i, peer in enumerate(peers):
        small(dest_ref, dest_all.at[me], dest_recv.at[me], (group, peer), i)

    piece = depth // PIECES

    def part(ref, j):
        return ref.at[pl.ds(j * piece, piece), :]

    def send(src, block, j, where, cond=None):
        number = count[0]
        count[0] += 1
        copy = pltpu.make_async_remote_copy(
            src_ref=part(src, j), dst_ref=part(wbuf.at[block], j),
            send_sem=w_send.at[number], recv_sem=w_recv.at[block, j],
            device_id=where, device_id_type=MESH,
        )
        pending.append((cond, copy))
        if cond is None:
            copy.start()
        else:
            pl.when(cond)(copy.start)

    def arrive(block, j):
        pltpu.make_async_remote_copy(
            src_ref=part(wbuf.at[block], j), dst_ref=part(wbuf.at[block], j),
            send_sem=w_send.at[0], recv_sem=w_recv.at[block, j],
            device_id=partner, device_id_type=MESH,
        ).wait_recv()

    def multiply(block):
        columns = pl.ds(pl.multiple_of(block * depth, depth), depth)
        acc[...] += jnp.dot(hid[:, columns], wbuf[block], preferred_element_type=jnp.float32)

    def origin(k):
        low = jnp.minimum(z, nz - 1 - z)
        near = z - 1 - k // 2 if k % 2 == 0 else z + 1 + k // 2
        rest = jnp.where(z == low, k + 1, nz - 2 - k)
        return jnp.where(k < 2 * low, near, rest)

    units = [(z, True), (z, False)]
    for k in range(nz - 1):
        units += [(origin(k), True), (origin(k), False)]

    def take_mine(i):
        zz, own = units[i]
        block = block_of(zz, y, x, c) if own else block_of(zz, y1, x1, c)
        for j in range(PIECES):
            if i == 0:
                src = w_hbm
            else:
                src = wbuf.at[block]
                arrive(block, j)
            if i < 2:
                up, down = z < nz - 1, z > 0
                if i == 1 and nz == 2:
                    up, down = z < 0, z < 0
                send(src, block, j, dev(jnp.minimum(z + 1, nz - 1), y, x, c), up)
                send(src, block, j, dev(jnp.maximum(z - 1, 0), y, x, c), down)
                if i == 0:
                    send(src, block, j, first)
            else:
                ahead = jnp.where(zz < z, z + 1, z - 1)
                inside = (ahead >= 0) & (ahead <= nz - 1)
                span = jnp.where(zz < z, z - zz, zz - z)
                target = jnp.clip(ahead, 0, nz - 1)
                if own:
                    send(src, block, j, dev(target, y, x, c), inside)
                    send(src, block, j, first, span == nz - 1)
                else:
                    send(src, block, j, dev(target, y, x, c), inside & (span + 1 < nz - 1))
            send(src, block, j, third)
            send(src, block, j, partner)
        if i == 0:
            return
        multiply(block)

    def take_third(i):
        zz, own = units[i]
        block = block_of(zz, y3, x3, c) if own else block_of(zz, yo, xo, c)
        for j in range(PIECES):
            arrive(block, j)
            send(wbuf.at[block], block, j, partner)
        multiply(block)

    def take_partner(i, far):
        zz, own = units[i]
        if far:
            block = block_of(zz, y1, x1, 1 - c) if own else block_of(zz, yo, xo, 1 - c)
        else:
            block = block_of(zz, y, x, 1 - c) if own else block_of(zz, y3, x3, 1 - c)
        for j in range(PIECES):
            arrive(block, j)
        multiply(block)

    def column(row):
        size = row.shape[1]
        a = lax.broadcasted_iota(jnp.int32, (size, size), 0)
        b = lax.broadcasted_iota(jnp.int32, (size, size), 1)
        return jnp.sum(jnp.where(a == b, row, 0.0), axis=1, keepdims=True)

    def send_queries():
        load_q.wait()
        row = dest_ref[...].astype(jnp.float32)
        col = column(row)
        a = lax.broadcasted_iota(jnp.int32, (rows, rows), 0)
        b = lax.broadcasted_iota(jnp.int32, (rows, rows), 1)
        rank = jnp.sum(jnp.where((col == row) & (a < b), 1.0, 0.0), axis=0, keepdims=True)
        slot = row * slots + rank
        number = lax.broadcasted_iota(jnp.int32, (n_seq * slots, rows), 0).astype(jnp.float32)
        select = jnp.where(number == slot, 1.0, 0.0).astype(jnp.bfloat16)
        moved = jnp.dot(select, qry[...], preferred_element_type=jnp.float32)
        outgoing[...] = moved.astype(jnp.bfloat16).reshape(outgoing.shape)
        for i, peer in enumerate(peers):
            small(outgoing.at[peer], received.at[me], qry_recv.at[me], (group, peer), n_seq + i)
        dest_all[me] = dest_ref[...]
        received[me] = outgoing[me]

    def wait_small(buffer, sems):
        for peer in peers:
            pltpu.make_async_remote_copy(
                src_ref=buffer.at[peer], dst_ref=buffer.at[peer], send_sem=small_send.at[0],
                recv_sem=sems.at[peer], device_id=partner, device_id_type=MESH,
            ).wait_recv()

    def prepare():
        wait_small(dest_all, dest_recv)
        wait_small(received, qry_recv)
        every = [dest_all[i].astype(jnp.float32) for i in range(n_seq)]
        row = jnp.concatenate(every, axis=1)
        a = lax.broadcasted_iota(jnp.int32, (rows, keys), 0)
        b = lax.broadcasted_iota(jnp.int32, (rows, keys), 1)
        position = jnp.zeros((1, keys), jnp.float32)
        for i in range(n_seq):
            col = column(every[i])
            before = (col < row) | ((col == row) & (a + i * rows < b))
            position += jnp.sum(jnp.where(before, 1.0, 0.0), axis=0, keepdims=True)
        segment = seg_ref[...].astype(jnp.float32)
        own_pos = a + me * rows
        own_seg = jnp.sum(jnp.where(own_pos == b, segment, 0.0), axis=1, keepdims=True)
        low = jnp.sum(jnp.where(segment < own_seg, 1.0, 0.0), axis=1, keepdims=True)
        allow = (position >= low) & (position <= own_pos.astype(jnp.float32))
        bias[...] = jnp.where(allow, 0.0, -1e30)
        width = n_seq * slots
        lane = lax.broadcasted_iota(jnp.int32, (1, width), 1)
        start = jnp.zeros((1, 1), jnp.float32)
        target = jnp.zeros((1, width), jnp.float32)
        mine_f = me.astype(jnp.float32)
        for i in range(n_seq):
            amount = jnp.sum(jnp.where(every[i] == mine_f, 1.0, 0.0), axis=1, keepdims=True)
            slot = (lane - i * slots).astype(jnp.float32)
            inside = (slot >= 0.0) & (slot < slots)
            target = jnp.where(inside, jnp.where(slot < amount, start + slot, -1.0), target)
            start = start + amount
        place_row = lax.broadcasted_iota(jnp.int32, (rows, width), 0).astype(jnp.float32)
        placer = jnp.where(place_row == target, 1.0, 0.0).astype(jnp.bfloat16)
        arrived = received[...].reshape(width, GROUP * HEAD)
        packed[...] = jnp.dot(placer, arrived, preferred_element_type=jnp.float32).astype(jnp.bfloat16)

    acc[...] = jnp.zeros_like(acc)
    last = len(units)
    for i in range(last + 2):
        if i < last:
            take_mine(i)
        if i == 0:
            send_queries()
            load_w.wait()
            load_h.wait()
            multiply(mine)
        if i == 3:
            prepare()
        if 0 <= i - 1 < last:
            take_third(i - 1)
            take_partner(i - 1, False)
        if 0 <= i - 2 < last:
            take_partner(i - 2, True)

    kv_all[me] = acc[...].astype(jnp.bfloat16)
    for i, peer in enumerate(peers):
        small(kv_all.at[me], kv_all.at[me], kv_recv.at[me], (group, peer), 2 * n_seq + i)
    wait_small(kv_all, kv_recv)

    scale = 1.0 / HEAD**0.5
    key = kv_all[:, :, :HEAD].reshape(keys, HEAD)
    value = kv_all[:, :, HEAD:].reshape(keys, HEAD)
    for h in range(GROUP):
        cols = pl.ds(h * HEAD, HEAD)
        scores = lax.dot_general(
            packed[:, cols], key, (((1,), (1,)), ((), ())), preferred_element_type=jnp.float32
        )
        scores = scores * scale + bias[...]
        top = jnp.max(scores, axis=1, keepdims=True)
        weights = jnp.exp(scores - top)
        total = jnp.sum(weights, axis=1, keepdims=True)
        numer = jnp.dot(weights.astype(jnp.bfloat16), value, preferred_element_type=jnp.float32)
        out_ref[:, cols] = (numer / total).astype(jnp.bfloat16)

    for cond, copy in pending:
        if cond is None:
            copy.wait_send()
        else:
            pl.when(cond)(copy.wait_send)


def fused_shards(hidden, queries, kv_weight, dest_device, segment_ids):
    n_seq, n_dp = lax.axis_size("seq"), lax.axis_size("dp")
    ny, nx = 2, n_seq // 2
    nz = n_dp // ny
    rows, d_model = hidden.shape
    depth, width = kv_weight.shape
    blocks = n_dp * n_seq
    width_q = queries.shape[1]
    keys = n_seq * rows
    dma = pltpu.SemaphoreType.DMA
    anyspace = pl.BlockSpec(memory_space=pl.ANY)
    vmem = pl.BlockSpec(memory_space=pltpu.VMEM)
    bf16, f32 = jnp.bfloat16, jnp.float32
    return pl.pallas_call(
        functools.partial(fused, nz, ny, nx),
        out_shape=jax.ShapeDtypeStruct((rows, width_q), bf16),
        in_specs=[anyspace, anyspace, anyspace, vmem, vmem],
        out_specs=vmem,
        scratch_shapes=[
            pltpu.VMEM((rows, d_model), bf16),
            pltpu.VMEM((rows, width_q), bf16),
            pltpu.VMEM((blocks, depth, width), bf16),
            pltpu.VMEM((n_seq, rows // 4, width_q), bf16),
            pltpu.VMEM((n_seq, rows // 4, width_q), bf16),
            pltpu.VMEM((n_seq, 1, rows), jnp.int32),
            pltpu.VMEM((n_seq, rows, width), bf16),
            pltpu.VMEM((rows, width_q), bf16),
            pltpu.VMEM((rows, keys), f32),
            pltpu.VMEM((rows, width), f32),
            dma((3,)),
            dma((PIECES * (9 + 9 * nz),)),
            dma((blocks, PIECES)),
            dma((3 * n_seq,)),
            dma((n_seq,)),
            dma((n_seq,)),
            dma((n_seq,)),
        ],
        compiler_params=pltpu.CompilerParams(
            collective_id=0, has_side_effects=True, vmem_limit_bytes=32 * 1024 * 1024
        ),
    )(hidden, queries, kv_weight, dest_device.reshape(1, rows), segment_ids)


def solution(mesh):
    in_specs = (
        P(("dp", "seq"), None),
        P(("dp", "seq"), None),
        P(("dp", "seq"), None),
        P(("dp", "seq")),
        P("dp", None),
    )
    out_specs = P(("dp", "seq"), None)
    n_dp, n_seq = mesh.shape["dp"], mesh.shape["seq"]
    body = fused_shards if n_seq == 4 and n_dp % 2 == 0 and 4 <= n_dp <= 16 else shards
    return jax.shard_map(body, mesh=mesh, in_specs=in_specs, out_specs=out_specs, check_vma=False)
```

```python
import functools

import jax
import jax.numpy as jnp
from jax import lax
from jax.experimental import pallas as pl
from jax.experimental.pallas import tpu as pltpu
from jax.sharding import PartitionSpec as P

HEAD = 128
GROUP = 8
PIECES = 2
FAR = 2
LAGS = (2, 2, 3)
MESH = pl.DeviceIdType.MESH


def shifted(shard, axis, by):
    devices = lax.axis_size(axis)
    pairs = [(i, i + by) for i in range(devices) if 0 <= i + by < devices]
    return lax.ppermute(shard, axis, pairs)


def shards(hidden, queries, kv_weight, dest_device, segment_ids):
    rows_dev = hidden.shape[0]
    width_q = GROUP * HEAD
    seq_count = lax.axis_size("seq")
    mine_index = lax.axis_index("seq")
    slots = rows_dev // 4
    reach = seq_count // 2
    scale = 1.0 / HEAD**0.5
    whole_weight = lax.all_gather(kv_weight, ("dp", "seq"), axis=0, tiled=True)
    kv_sum = jnp.dot(hidden, whole_weight, preferred_element_type=jnp.float32)
    kv_vals = kv_sum.astype(jnp.bfloat16)
    feats = jnp.concatenate([queries, kv_vals], axis=1)
    lanes = jnp.arange(seq_count, dtype=jnp.int32)
    offsets = (dest_device - mine_index) % seq_count
    member = (offsets[:, None] == lanes[None, :]).astype(jnp.int32)
    counts = jnp.sum(member, axis=0)
    dest_member = (dest_device[:, None] == lanes[None, :]).astype(jnp.int32)
    rank_in = jnp.sum((jnp.cumsum(dest_member, axis=0) - 1) * dest_member, axis=1)
    send_slot = dest_device * slots + rank_in
    select = (jnp.arange(seq_count * slots, dtype=jnp.int32)[:, None] == send_slot[None, :]).astype(
        jnp.bfloat16
    )
    outgoing = jnp.dot(select, feats, preferred_element_type=jnp.float32).astype(jnp.bfloat16)
    outgoing = outgoing.reshape(seq_count, slots, feats.shape[1])
    received = lax.all_to_all(outgoing, "seq", split_axis=0, concat_axis=0, tiled=True).reshape(
        seq_count * slots, feats.shape[1]
    )
    lookup = ((mine_index - lanes) % seq_count)[:, None] == lanes[None, :]
    from_count = jnp.sum(jnp.where(lookup, counts[None, :], 0), axis=1)
    from_start = jnp.cumsum(from_count) - from_count
    slot_index = jnp.broadcast_to(jnp.arange(slots, dtype=jnp.int32)[None, :], (seq_count, slots))
    dest_pos = (from_start[:, None] + slot_index).reshape(-1)
    valid = (slot_index < from_count[:, None]).reshape(-1)
    placer = (
        (jnp.arange(rows_dev, dtype=jnp.int32)[:, None] == dest_pos[None, :]) & valid[None, :]
    ).astype(jnp.bfloat16)
    packed = jnp.dot(placer, received, preferred_element_type=jnp.float32).astype(jnp.bfloat16)
    query_rows = packed[:, :width_q].reshape(rows_dev, GROUP, HEAD)
    kv_local = packed[:, width_q:]
    seg_row = segment_ids[0]
    own_start = mine_index * rows_dev
    query_seg = lax.dynamic_slice_in_dim(seg_row, own_start, rows_dev, 0)
    query_pos = own_start + jnp.arange(rows_dev, dtype=jnp.int32)

    def attend(carry, piece, start):
        top_old, total_old, numer_old = carry
        count_keys = piece.shape[0]
        key_pos = start + jnp.arange(count_keys, dtype=jnp.int32)
        key_seg = lax.dynamic_slice_in_dim(seg_row, jnp.maximum(start, 0), count_keys, 0)
        allow = (
            (query_seg[:, None] == key_seg[None, :])
            & (key_pos[None, :] <= query_pos[:, None])
            & (key_pos[None, :] >= 0)
        )
        allow = allow[None, :, :]
        scores = (
            jnp.einsum(
                "rgh,kh->grk", query_rows, piece[:, :HEAD], preferred_element_type=jnp.float32
            )
            * scale
        )
        top_new = jnp.maximum(top_old, jnp.max(jnp.where(allow, scores, -1e30), axis=-1))
        weights = jnp.where(allow, jnp.exp(scores - top_new[:, :, None]), 0.0)
        factor = jnp.exp(top_old - top_new)
        total_new = total_old * factor + jnp.sum(weights, axis=-1)
        contrib = jnp.einsum(
            "grk,kh->grh",
            weights.astype(jnp.bfloat16),
            piece[:, HEAD:],
            preferred_element_type=jnp.float32,
        )
        numer_new = numer_old * factor[:, :, None] + contrib
        return (top_new, total_new, numer_new)

    start_carry = (
        jnp.full((GROUP, rows_dev), -1e30, jnp.float32),
        jnp.zeros((GROUP, rows_dev), jnp.float32),
        jnp.zeros((GROUP, rows_dev, HEAD), jnp.float32),
    )
    state = attend(start_carry, kv_local, own_start)
    for back in range(1, reach + 1):
        earlier = shifted(kv_local, "seq", back)
        state = attend(state, earlier, own_start - back * rows_dev)
    top_val, total, numer = state
    result = (numer / total[:, :, None]).astype(jnp.bfloat16)
    return jnp.transpose(result, (1, 0, 2)).reshape(rows_dev, width_q)


def fused(
    nz, ny, nx, hid_hbm, qry_hbm, w_hbm, dest_ref, seg_ref, out_ref,
    hid, qry, wbuf, outgoing, received, dest_all, kv_all, packed, bias, acc,
    load_sem, w_send, w_recv, small_send, dest_recv, qry_recv, kv_recv,
):
    rows = hid.shape[0]
    depth = wbuf.shape[1]
    n_seq = nx * 2
    far = FAR
    slots = rows // 4
    keys = n_seq * rows
    group = lax.axis_index("dp")
    me = lax.axis_index("seq")
    z, y = lax.div(group, ny), lax.rem(group, ny)
    x, c = lax.div(me, 2), lax.rem(me, 2)
    x1, y1 = x + (1 - c) * (1 - 2 * x), y + c * (1 - 2 * y)
    x3, y3 = x + c * (1 - 2 * x), y + (1 - c) * (1 - 2 * y)
    xo, yo = 1 - x, 1 - y

    def dev(zz, yy, xx, cc):
        return (zz * ny + yy, xx * 2 + cc)

    def block_of(zz, yy, xx, cc):
        return (zz * ny + yy) * n_seq + xx * 2 + cc

    first, third = dev(z, y1, x1, c), dev(z, y3, x3, c)
    partner = dev(z, y, x, 1 - c)
    peers = [lax.rem(me + i, n_seq) for i in range(1, n_seq)]

    mine = block_of(z, y, x, c)
    load_q = pltpu.make_async_copy(qry_hbm, qry, load_sem.at[0])
    load_w = pltpu.make_async_copy(w_hbm, wbuf.at[mine], load_sem.at[1])
    load_h = pltpu.make_async_copy(hid_hbm, hid, load_sem.at[2])
    load_q.start()
    load_w.start()
    load_h.start()

    barrier = pltpu.get_barrier_semaphore()
    for peer in peers:
        pl.semaphore_signal(barrier, inc=1, device_id=(group, peer), device_id_type=MESH)
    pl.semaphore_signal(barrier, inc=1, device_id=dev(z, yo, x, c), device_id_type=MESH)

    @pl.when(z > 0)
    def _():
        pl.semaphore_signal(barrier, inc=1, device_id=dev(z - 1, y, x, c), device_id_type=MESH)

    @pl.when(z < nz - 1)
    def _():
        pl.semaphore_signal(barrier, inc=1, device_id=dev(z + 1, y, x, c), device_id_type=MESH)

    above, below = (z < nz - 1).astype(jnp.int32), (z > 0).astype(jnp.int32)
    pl.semaphore_wait(barrier, n_seq + above + below)

    pending = []
    count = [0]

    def small(src, dst, recv, where, number):
        copy = pltpu.make_async_remote_copy(
            src_ref=src, dst_ref=dst, send_sem=small_send.at[number], recv_sem=recv,
            device_id=where, device_id_type=MESH,
        )
        copy.start()
        pending.append((None, copy))

    for i, peer in enumerate(peers):
        small(dest_ref, dest_all.at[me], dest_recv.at[me], (group, peer), i)

    piece = depth // PIECES

    def part(ref, j):
        return ref.at[pl.ds(j * piece, piece), :]

    def send(src, block, j, where, cond=None):
        number = count[0]
        count[0] += 1
        copy = pltpu.make_async_remote_copy(
            src_ref=part(src, j), dst_ref=part(wbuf.at[block], j),
            send_sem=w_send.at[number], recv_sem=w_recv.at[block, j],
            device_id=where, device_id_type=MESH,
        )
        pending.append((cond, copy))
        if cond is None:
            copy.start()
        else:
            pl.when(cond)(copy.start)

    def arrive(block, j):
        pltpu.make_async_remote_copy(
            src_ref=part(wbuf.at[block], j), dst_ref=part(wbuf.at[block], j),
            send_sem=w_send.at[0], recv_sem=w_recv.at[block, j],
            device_id=partner, device_id_type=MESH,
        ).wait_recv()

    def multiply(block):
        columns = pl.ds(pl.multiple_of(block * depth, depth), depth)
        acc[...] += jnp.dot(hid[:, columns], wbuf[block], preferred_element_type=jnp.float32)

    def origin(k):
        low = jnp.minimum(z, nz - 1 - z)
        near = z - 1 - k // 2 if k % 2 == 0 else z + 1 + k // 2
        rest = jnp.where(z == low, k + 1, nz - 2 - k)
        return jnp.where(k < 2 * low, near, rest)

    units = [(z, True), (z, False)]
    for k in range(nz - 1):
        units += [(origin(k), True), (origin(k), False)]

    def take_mine(i):
        zz, own = units[i]
        block = block_of(zz, y, x, c) if own else block_of(zz, y1, x1, c)
        for j in range(PIECES):
            if i == 0:
                src = w_hbm
            else:
                src = wbuf.at[block]
                arrive(block, j)
            if i < 2:
                up, down = z < nz - 1, z > 0
                if i == 1 and far < 2:
                    up, down = z < 0, z < 0
                send(src, block, j, dev(jnp.minimum(z + 1, nz - 1), y, x, c), up)
                send(src, block, j, dev(jnp.maximum(z - 1, 0), y, x, c), down)
                if i == 0:
                    send(src, block, j, first)
            else:
                ahead = jnp.where(zz < z, z + 1, z - 1)
                inside = (ahead >= 0) & (ahead <= nz - 1)
                span = jnp.where(zz < z, z - zz, zz - z)
                target = jnp.clip(ahead, 0, nz - 1)
                if own:
                    send(src, block, j, dev(target, y, x, c), inside)
                    send(src, block, j, first, span >= far)
                else:
                    send(src, block, j, dev(target, y, x, c), inside & (span + 1 < far))
            send(src, block, j, third)
            send(src, block, j, partner)
        if i == 0:
            return
        multiply(block)

    def take_third(i):
        zz, own = units[i]
        block = block_of(zz, y3, x3, c) if own else block_of(zz, yo, xo, c)
        for j in range(PIECES):
            arrive(block, j)
            send(wbuf.at[block], block, j, partner)
        multiply(block)

    def take_partner(i, far):
        zz, own = units[i]
        if far:
            block = block_of(zz, y1, x1, 1 - c) if own else block_of(zz, yo, xo, 1 - c)
        else:
            block = block_of(zz, y, x, 1 - c) if own else block_of(zz, y3, x3, 1 - c)
        for j in range(PIECES):
            arrive(block, j)
        multiply(block)

    def column(row):
        size = row.shape[1]
        a = lax.broadcasted_iota(jnp.int32, (size, size), 0)
        b = lax.broadcasted_iota(jnp.int32, (size, size), 1)
        return jnp.sum(jnp.where(a == b, row, 0.0), axis=1, keepdims=True)

    def send_queries():
        load_q.wait()
        row = dest_ref[...].astype(jnp.float32)
        col = column(row)
        a = lax.broadcasted_iota(jnp.int32, (rows, rows), 0)
        b = lax.broadcasted_iota(jnp.int32, (rows, rows), 1)
        rank = jnp.sum(jnp.where((col == row) & (a < b), 1.0, 0.0), axis=0, keepdims=True)
        slot = row * slots + rank
        number = lax.broadcasted_iota(jnp.int32, (n_seq * slots, rows), 0).astype(jnp.float32)
        select = jnp.where(number == slot, 1.0, 0.0).astype(jnp.bfloat16)
        moved = jnp.dot(select, qry[...], preferred_element_type=jnp.float32)
        outgoing[...] = moved.astype(jnp.bfloat16).reshape(outgoing.shape)
        for i, peer in enumerate(peers):
            small(outgoing.at[peer], received.at[me], qry_recv.at[me], (group, peer), n_seq + i)
        dest_all[me] = dest_ref[...]
        received[me] = outgoing[me]

    def wait_small(buffer, sems):
        for peer in peers:
            pltpu.make_async_remote_copy(
                src_ref=buffer.at[peer], dst_ref=buffer.at[peer], send_sem=small_send.at[0],
                recv_sem=sems.at[peer], device_id=partner, device_id_type=MESH,
            ).wait_recv()

    def prepare():
        wait_small(dest_all, dest_recv)
        wait_small(received, qry_recv)
        every = [dest_all[i].astype(jnp.float32) for i in range(n_seq)]
        row = jnp.concatenate(every, axis=1)
        a = lax.broadcasted_iota(jnp.int32, (rows, keys), 0)
        b = lax.broadcasted_iota(jnp.int32, (rows, keys), 1)
        position = jnp.zeros((1, keys), jnp.float32)
        for i in range(n_seq):
            col = column(every[i])
            before = (col < row) | ((col == row) & (a + i * rows < b))
            position += jnp.sum(jnp.where(before, 1.0, 0.0), axis=0, keepdims=True)
        segment = seg_ref[...].astype(jnp.float32)
        own_pos = a + me * rows
        own_seg = jnp.sum(jnp.where(own_pos == b, segment, 0.0), axis=1, keepdims=True)
        low = jnp.sum(jnp.where(segment < own_seg, 1.0, 0.0), axis=1, keepdims=True)
        allow = (position >= low) & (position <= own_pos.astype(jnp.float32))
        bias[...] = jnp.where(allow, 0.0, -1e30)
        width = n_seq * slots
        lane = lax.broadcasted_iota(jnp.int32, (1, width), 1)
        start = jnp.zeros((1, 1), jnp.float32)
        target = jnp.zeros((1, width), jnp.float32)
        mine_f = me.astype(jnp.float32)
        for i in range(n_seq):
            amount = jnp.sum(jnp.where(every[i] == mine_f, 1.0, 0.0), axis=1, keepdims=True)
            slot = (lane - i * slots).astype(jnp.float32)
            inside = (slot >= 0.0) & (slot < slots)
            target = jnp.where(inside, jnp.where(slot < amount, start + slot, -1.0), target)
            start = start + amount
        place_row = lax.broadcasted_iota(jnp.int32, (rows, width), 0).astype(jnp.float32)
        placer = jnp.where(place_row == target, 1.0, 0.0).astype(jnp.bfloat16)
        arrived = received[...].reshape(width, GROUP * HEAD)
        packed[...] = jnp.dot(placer, arrived, preferred_element_type=jnp.float32).astype(jnp.bfloat16)

    acc[...] = jnp.zeros_like(acc)
    last = len(units)
    lag_third, lag_near, lag_far = LAGS
    for i in range(last + max(LAGS)):
        if i < last:
            take_mine(i)
        if i == 0:
            send_queries()
            load_w.wait()
            load_h.wait()
            multiply(mine)
        if i == 3:
            prepare()
        if 0 <= i - lag_third < last:
            take_third(i - lag_third)
        if 0 <= i - lag_near < last:
            take_partner(i - lag_near, False)
        if 0 <= i - lag_far < last:
            take_partner(i - lag_far, True)

    kv_all[me] = acc[...].astype(jnp.bfloat16)
    for i, peer in enumerate(peers):
        small(kv_all.at[me], kv_all.at[me], kv_recv.at[me], (group, peer), 2 * n_seq + i)
    wait_small(kv_all, kv_recv)

    scale = 1.0 / HEAD**0.5
    key = kv_all[:, :, :HEAD].reshape(keys, HEAD)
    value = kv_all[:, :, HEAD:].reshape(keys, HEAD)
    for h in range(GROUP):
        cols = pl.ds(h * HEAD, HEAD)
        scores = lax.dot_general(
            packed[:, cols], key, (((1,), (1,)), ((), ())), preferred_element_type=jnp.float32
        )
        scores = scores * scale + bias[...]
        top = jnp.max(scores, axis=1, keepdims=True)
        weights = jnp.exp(scores - top)
        total = jnp.sum(weights, axis=1, keepdims=True)
        numer = jnp.dot(weights.astype(jnp.bfloat16), value, preferred_element_type=jnp.float32)
        out_ref[:, cols] = (numer / total).astype(jnp.bfloat16)

    for cond, copy in pending:
        if cond is None:
            copy.wait_send()
        else:
            pl.when(cond)(copy.wait_send)


def fused_shards(hidden, queries, kv_weight, dest_device, segment_ids):
    n_seq, n_dp = lax.axis_size("seq"), lax.axis_size("dp")
    ny, nx = 2, n_seq // 2
    nz = n_dp // ny
    rows, d_model = hidden.shape
    depth, width = kv_weight.shape
    blocks = n_dp * n_seq
    width_q = queries.shape[1]
    keys = n_seq * rows
    dma = pltpu.SemaphoreType.DMA
    anyspace = pl.BlockSpec(memory_space=pl.ANY)
    vmem = pl.BlockSpec(memory_space=pltpu.VMEM)
    bf16, f32 = jnp.bfloat16, jnp.float32
    return pl.pallas_call(
        functools.partial(fused, nz, ny, nx),
        out_shape=jax.ShapeDtypeStruct((rows, width_q), bf16),
        in_specs=[anyspace, anyspace, anyspace, vmem, vmem],
        out_specs=vmem,
        scratch_shapes=[
            pltpu.VMEM((rows, d_model), bf16),
            pltpu.VMEM((rows, width_q), bf16),
            pltpu.VMEM((blocks, depth, width), bf16),
            pltpu.VMEM((n_seq, rows // 4, width_q), bf16),
            pltpu.VMEM((n_seq, rows // 4, width_q), bf16),
            pltpu.VMEM((n_seq, 1, rows), jnp.int32),
            pltpu.VMEM((n_seq, rows, width), bf16),
            pltpu.VMEM((rows, width_q), bf16),
            pltpu.VMEM((rows, keys), f32),
            pltpu.VMEM((rows, width), f32),
            dma((3,)),
            dma((PIECES * (9 + 9 * nz),)),
            dma((blocks, PIECES)),
            dma((3 * n_seq,)),
            dma((n_seq,)),
            dma((n_seq,)),
            dma((n_seq,)),
        ],
        compiler_params=pltpu.CompilerParams(
            collective_id=0, has_side_effects=True, vmem_limit_bytes=32 * 1024 * 1024
        ),
    )(hidden, queries, kv_weight, dest_device.reshape(1, rows), segment_ids)


def solution(mesh):
    in_specs = (
        P(("dp", "seq"), None),
        P(("dp", "seq"), None),
        P(("dp", "seq"), None),
        P(("dp", "seq")),
        P("dp", None),
    )
    out_specs = P(("dp", "seq"), None)
    n_dp, n_seq = mesh.shape["dp"], mesh.shape["seq"]
    body = fused_shards if n_seq == 4 and n_dp % 2 == 0 and 4 <= n_dp <= 16 else shards
    return jax.shard_map(body, mesh=mesh, in_specs=in_specs, out_specs=out_specs, check_vma=False)
```

```python
import functools

import jax
import jax.numpy as jnp
from jax import lax
from jax.experimental import pallas as pl
from jax.experimental.pallas import tpu as pltpu
from jax.sharding import PartitionSpec as P

HEAD = 128
GROUP = 8
PIECES = 2
FAR = 2
LAGS = (2, 2, 3)
MESH = pl.DeviceIdType.MESH


def shifted(shard, axis, by):
    devices = lax.axis_size(axis)
    pairs = [(i, i + by) for i in range(devices) if 0 <= i + by < devices]
    return lax.ppermute(shard, axis, pairs)


def shards(hidden, queries, kv_weight, dest_device, segment_ids):
    rows_dev = hidden.shape[0]
    width_q = GROUP * HEAD
    seq_count = lax.axis_size("seq")
    mine_index = lax.axis_index("seq")
    slots = rows_dev // 4
    reach = seq_count // 2
    scale = 1.0 / HEAD**0.5
    whole_weight = lax.all_gather(kv_weight, ("dp", "seq"), axis=0, tiled=True)
    kv_sum = jnp.dot(hidden, whole_weight, preferred_element_type=jnp.float32)
    kv_vals = kv_sum.astype(jnp.bfloat16)
    feats = jnp.concatenate([queries, kv_vals], axis=1)
    lanes = jnp.arange(seq_count, dtype=jnp.int32)
    offsets = (dest_device - mine_index) % seq_count
    member = (offsets[:, None] == lanes[None, :]).astype(jnp.int32)
    counts = jnp.sum(member, axis=0)
    dest_member = (dest_device[:, None] == lanes[None, :]).astype(jnp.int32)
    rank_in = jnp.sum((jnp.cumsum(dest_member, axis=0) - 1) * dest_member, axis=1)
    send_slot = dest_device * slots + rank_in
    select = (jnp.arange(seq_count * slots, dtype=jnp.int32)[:, None] == send_slot[None, :]).astype(
        jnp.bfloat16
    )
    outgoing = jnp.dot(select, feats, preferred_element_type=jnp.float32).astype(jnp.bfloat16)
    outgoing = outgoing.reshape(seq_count, slots, feats.shape[1])
    received = lax.all_to_all(outgoing, "seq", split_axis=0, concat_axis=0, tiled=True).reshape(
        seq_count * slots, feats.shape[1]
    )
    lookup = ((mine_index - lanes) % seq_count)[:, None] == lanes[None, :]
    from_count = jnp.sum(jnp.where(lookup, counts[None, :], 0), axis=1)
    from_start = jnp.cumsum(from_count) - from_count
    slot_index = jnp.broadcast_to(jnp.arange(slots, dtype=jnp.int32)[None, :], (seq_count, slots))
    dest_pos = (from_start[:, None] + slot_index).reshape(-1)
    valid = (slot_index < from_count[:, None]).reshape(-1)
    placer = (
        (jnp.arange(rows_dev, dtype=jnp.int32)[:, None] == dest_pos[None, :]) & valid[None, :]
    ).astype(jnp.bfloat16)
    packed = jnp.dot(placer, received, preferred_element_type=jnp.float32).astype(jnp.bfloat16)
    query_rows = packed[:, :width_q].reshape(rows_dev, GROUP, HEAD)
    kv_local = packed[:, width_q:]
    seg_row = segment_ids[0]
    own_start = mine_index * rows_dev
    query_seg = lax.dynamic_slice_in_dim(seg_row, own_start, rows_dev, 0)
    query_pos = own_start + jnp.arange(rows_dev, dtype=jnp.int32)

    def attend(carry, piece, start):
        top_old, total_old, numer_old = carry
        count_keys = piece.shape[0]
        key_pos = start + jnp.arange(count_keys, dtype=jnp.int32)
        key_seg = lax.dynamic_slice_in_dim(seg_row, jnp.maximum(start, 0), count_keys, 0)
        allow = (
            (query_seg[:, None] == key_seg[None, :])
            & (key_pos[None, :] <= query_pos[:, None])
            & (key_pos[None, :] >= 0)
        )
        allow = allow[None, :, :]
        scores = (
            jnp.einsum(
                "rgh,kh->grk", query_rows, piece[:, :HEAD], preferred_element_type=jnp.float32
            )
            * scale
        )
        top_new = jnp.maximum(top_old, jnp.max(jnp.where(allow, scores, -1e30), axis=-1))
        weights = jnp.where(allow, jnp.exp(scores - top_new[:, :, None]), 0.0)
        factor = jnp.exp(top_old - top_new)
        total_new = total_old * factor + jnp.sum(weights, axis=-1)
        contrib = jnp.einsum(
            "grk,kh->grh",
            weights.astype(jnp.bfloat16),
            piece[:, HEAD:],
            preferred_element_type=jnp.float32,
        )
        numer_new = numer_old * factor[:, :, None] + contrib
        return (top_new, total_new, numer_new)

    start_carry = (
        jnp.full((GROUP, rows_dev), -1e30, jnp.float32),
        jnp.zeros((GROUP, rows_dev), jnp.float32),
        jnp.zeros((GROUP, rows_dev, HEAD), jnp.float32),
    )
    state = attend(start_carry, kv_local, own_start)
    for back in range(1, reach + 1):
        earlier = shifted(kv_local, "seq", back)
        state = attend(state, earlier, own_start - back * rows_dev)
    top_val, total, numer = state
    result = (numer / total[:, :, None]).astype(jnp.bfloat16)
    return jnp.transpose(result, (1, 0, 2)).reshape(rows_dev, width_q)


def fused(
    nz, ny, nx, hid_hbm, qry_hbm, w_hbm, dest_ref, seg_ref, out_ref,
    hid, qry, wbuf, outgoing, received, dest_all, kv_all, packed, bias, acc, tops, totals, numers,
    load_sem, w_send, w_recv, small_send, dest_recv, qry_recv, kv_recv,
):
    rows = hid.shape[0]
    depth = wbuf.shape[1]
    n_seq = nx * 2
    far = FAR
    slots = rows // 4
    keys = n_seq * rows
    group = lax.axis_index("dp")
    me = lax.axis_index("seq")
    z, y = lax.div(group, ny), lax.rem(group, ny)
    x, c = lax.div(me, 2), lax.rem(me, 2)
    x1, y1 = x + (1 - c) * (1 - 2 * x), y + c * (1 - 2 * y)
    x3, y3 = x + c * (1 - 2 * x), y + (1 - c) * (1 - 2 * y)
    xo, yo = 1 - x, 1 - y

    def dev(zz, yy, xx, cc):
        return (zz * ny + yy, xx * 2 + cc)

    def block_of(zz, yy, xx, cc):
        return (zz * ny + yy) * n_seq + xx * 2 + cc

    first, third = dev(z, y1, x1, c), dev(z, y3, x3, c)
    partner = dev(z, y, x, 1 - c)
    peers = [lax.rem(me + i, n_seq) for i in range(1, n_seq)]

    mine = block_of(z, y, x, c)
    load_q = pltpu.make_async_copy(qry_hbm, qry, load_sem.at[0])
    load_w = pltpu.make_async_copy(w_hbm, wbuf.at[mine], load_sem.at[1])
    load_h = pltpu.make_async_copy(hid_hbm, hid, load_sem.at[2])
    load_q.start()
    load_w.start()
    load_h.start()

    barrier = pltpu.get_barrier_semaphore()
    for peer in peers:
        pl.semaphore_signal(barrier, inc=1, device_id=(group, peer), device_id_type=MESH)
    pl.semaphore_signal(barrier, inc=1, device_id=dev(z, yo, x, c), device_id_type=MESH)

    @pl.when(z > 0)
    def _():
        pl.semaphore_signal(barrier, inc=1, device_id=dev(z - 1, y, x, c), device_id_type=MESH)

    @pl.when(z < nz - 1)
    def _():
        pl.semaphore_signal(barrier, inc=1, device_id=dev(z + 1, y, x, c), device_id_type=MESH)

    above, below = (z < nz - 1).astype(jnp.int32), (z > 0).astype(jnp.int32)
    pl.semaphore_wait(barrier, n_seq + above + below)

    pending = []
    count = [0]

    def small(src, dst, recv, where, number):
        copy = pltpu.make_async_remote_copy(
            src_ref=src, dst_ref=dst, send_sem=small_send.at[number], recv_sem=recv,
            device_id=where, device_id_type=MESH,
        )
        copy.start()
        pending.append((None, copy))

    for i, peer in enumerate(peers):
        small(dest_ref, dest_all.at[me], dest_recv.at[me], (group, peer), i)

    piece = depth // PIECES

    def part(ref, j):
        return ref.at[pl.ds(j * piece, piece), :]

    def send(src, block, j, where, cond=None):
        number = count[0]
        count[0] += 1
        copy = pltpu.make_async_remote_copy(
            src_ref=part(src, j), dst_ref=part(wbuf.at[block], j),
            send_sem=w_send.at[number], recv_sem=w_recv.at[block, j],
            device_id=where, device_id_type=MESH,
        )
        pending.append((cond, copy))
        if cond is None:
            copy.start()
        else:
            pl.when(cond)(copy.start)

    def arrive(block, j):
        pltpu.make_async_remote_copy(
            src_ref=part(wbuf.at[block], j), dst_ref=part(wbuf.at[block], j),
            send_sem=w_send.at[0], recv_sem=w_recv.at[block, j],
            device_id=partner, device_id_type=MESH,
        ).wait_recv()

    def multiply(block):
        columns = pl.ds(pl.multiple_of(block * depth, depth), depth)
        acc[...] += jnp.dot(hid[:, columns], wbuf[block], preferred_element_type=jnp.float32)

    def origin(k):
        low = jnp.minimum(z, nz - 1 - z)
        near = z - 1 - k // 2 if k % 2 == 0 else z + 1 + k // 2
        rest = jnp.where(z == low, k + 1, nz - 2 - k)
        return jnp.where(k < 2 * low, near, rest)

    units = [(z, True), (z, False)]
    for k in range(nz - 1):
        units += [(origin(k), True), (origin(k), False)]

    def take_mine(i):
        zz, own = units[i]
        block = block_of(zz, y, x, c) if own else block_of(zz, y1, x1, c)
        for j in range(PIECES):
            if i == 0:
                src = w_hbm
            else:
                src = wbuf.at[block]
                arrive(block, j)
            if i < 2:
                up, down = z < nz - 1, z > 0
                if i == 1 and far < 2:
                    up, down = z < 0, z < 0
                send(src, block, j, dev(jnp.minimum(z + 1, nz - 1), y, x, c), up)
                send(src, block, j, dev(jnp.maximum(z - 1, 0), y, x, c), down)
                if i == 0:
                    send(src, block, j, first)
            else:
                ahead = jnp.where(zz < z, z + 1, z - 1)
                inside = (ahead >= 0) & (ahead <= nz - 1)
                span = jnp.where(zz < z, z - zz, zz - z)
                target = jnp.clip(ahead, 0, nz - 1)
                if own:
                    send(src, block, j, dev(target, y, x, c), inside)
                    send(src, block, j, first, span >= far)
                else:
                    send(src, block, j, dev(target, y, x, c), inside & (span + 1 < far))
            send(src, block, j, third)
            send(src, block, j, partner)
        if i == 0:
            return
        multiply(block)

    def take_third(i):
        zz, own = units[i]
        block = block_of(zz, y3, x3, c) if own else block_of(zz, yo, xo, c)
        for j in range(PIECES):
            arrive(block, j)
            send(wbuf.at[block], block, j, partner)
        multiply(block)

    def take_partner(i, far):
        zz, own = units[i]
        if far:
            block = block_of(zz, y1, x1, 1 - c) if own else block_of(zz, yo, xo, 1 - c)
        else:
            block = block_of(zz, y, x, 1 - c) if own else block_of(zz, y3, x3, 1 - c)
        for j in range(PIECES):
            arrive(block, j)
        multiply(block)

    def column(row):
        size = row.shape[1]
        a = lax.broadcasted_iota(jnp.int32, (size, size), 0)
        b = lax.broadcasted_iota(jnp.int32, (size, size), 1)
        return jnp.sum(jnp.where(a == b, row, 0.0), axis=1, keepdims=True)

    def send_queries():
        load_q.wait()
        row = dest_ref[...].astype(jnp.float32)
        col = column(row)
        a = lax.broadcasted_iota(jnp.int32, (rows, rows), 0)
        b = lax.broadcasted_iota(jnp.int32, (rows, rows), 1)
        rank = jnp.sum(jnp.where((col == row) & (a < b), 1.0, 0.0), axis=0, keepdims=True)
        slot = row * slots + rank
        number = lax.broadcasted_iota(jnp.int32, (n_seq * slots, rows), 0).astype(jnp.float32)
        select = jnp.where(number == slot, 1.0, 0.0).astype(jnp.bfloat16)
        moved = jnp.dot(select, qry[...], preferred_element_type=jnp.float32)
        outgoing[...] = moved.astype(jnp.bfloat16).reshape(outgoing.shape)
        for i, peer in enumerate(peers):
            small(outgoing.at[peer], received.at[me], qry_recv.at[me], (group, peer), n_seq + i)
        dest_all[me] = dest_ref[...]
        received[me] = outgoing[me]

    def wait_small(buffer, sems):
        for peer in peers:
            pltpu.make_async_remote_copy(
                src_ref=buffer.at[peer], dst_ref=buffer.at[peer], send_sem=small_send.at[0],
                recv_sem=sems.at[peer], device_id=partner, device_id_type=MESH,
            ).wait_recv()

    def prepare():
        wait_small(dest_all, dest_recv)
        wait_small(received, qry_recv)
        every = [dest_all[i].astype(jnp.float32) for i in range(n_seq)]
        row = jnp.concatenate(every, axis=1)
        a = lax.broadcasted_iota(jnp.int32, (rows, keys), 0)
        b = lax.broadcasted_iota(jnp.int32, (rows, keys), 1)
        position = jnp.zeros((1, keys), jnp.float32)
        for i in range(n_seq):
            col = column(every[i])
            before = (col < row) | ((col == row) & (a + i * rows < b))
            position += jnp.sum(jnp.where(before, 1.0, 0.0), axis=0, keepdims=True)
        segment = seg_ref[...].astype(jnp.float32)
        own_pos = a + me * rows
        own_seg = jnp.sum(jnp.where(own_pos == b, segment, 0.0), axis=1, keepdims=True)
        low = jnp.sum(jnp.where(segment < own_seg, 1.0, 0.0), axis=1, keepdims=True)
        allow = (position >= low) & (position <= own_pos.astype(jnp.float32))
        bias[...] = jnp.where(allow, 0.0, -1e30)
        width = n_seq * slots
        lane = lax.broadcasted_iota(jnp.int32, (1, width), 1)
        start = jnp.zeros((1, 1), jnp.float32)
        target = jnp.zeros((1, width), jnp.float32)
        mine_f = me.astype(jnp.float32)
        for i in range(n_seq):
            amount = jnp.sum(jnp.where(every[i] == mine_f, 1.0, 0.0), axis=1, keepdims=True)
            slot = (lane - i * slots).astype(jnp.float32)
            inside = (slot >= 0.0) & (slot < slots)
            target = jnp.where(inside, jnp.where(slot < amount, start + slot, -1.0), target)
            start = start + amount
        place_row = lax.broadcasted_iota(jnp.int32, (rows, width), 0).astype(jnp.float32)
        placer = jnp.where(place_row == target, 1.0, 0.0).astype(jnp.bfloat16)
        arrived = received[...].reshape(width, GROUP * HEAD)
        packed[...] = jnp.dot(placer, arrived, preferred_element_type=jnp.float32).astype(jnp.bfloat16)

    acc[...] = jnp.zeros_like(acc)
    last = len(units)
    lag_third, lag_near, lag_far = LAGS
    for i in range(last + max(LAGS)):
        if i < last:
            take_mine(i)
        if i == 0:
            send_queries()
            load_w.wait()
            load_h.wait()
            multiply(mine)
        if i == 5:
            prepare()
        if 0 <= i - lag_third < last:
            take_third(i - lag_third)
        if 0 <= i - lag_near < last:
            take_partner(i - lag_near, False)
        if 0 <= i - lag_far < last:
            take_partner(i - lag_far, True)

    kv_all[me] = acc[...].astype(jnp.bfloat16)
    for i, peer in enumerate([lax.rem(x * 2 + j, n_seq) for j in range(2, n_seq)] + [x * 2 + 1 - c]):
        small(kv_all.at[me], kv_all.at[me], kv_recv.at[me], (group, peer), 2 * n_seq + i)
    scale = 1.0 / HEAD**0.5

    def attend(h, sources, state):
        cols = pl.ds(h * HEAD, HEAD)
        parts = []
        for source in sources:
            scores = lax.dot_general(
                packed[:, cols], kv_all[source, :, :HEAD], (((1,), (1,)), ((), ())),
                preferred_element_type=jnp.float32,
            )
            window = pl.ds(pl.multiple_of(source * rows, rows), rows)
            parts.append(scores * scale + bias[:, window])
        scores = jnp.concatenate(parts, axis=1)
        value = jnp.concatenate([kv_all[source, :, HEAD:] for source in sources], axis=0)
        top = jnp.max(scores, axis=1, keepdims=True)
        if state is not None:
            top = jnp.maximum(top, state[0])
        weights = jnp.exp(scores - top)
        total = jnp.sum(weights, axis=1, keepdims=True)
        numer = jnp.dot(weights.astype(jnp.bfloat16), value, preferred_element_type=jnp.float32)
        if state is not None:
            factor = jnp.exp(state[0] - top)
            total, numer = total + state[1] * factor, numer + state[2] * factor
        return top, total, numer

    def wait_kv(source):
        pltpu.make_async_remote_copy(
            src_ref=kv_all.at[source], dst_ref=kv_all.at[source], send_sem=small_send.at[0],
            recv_sem=kv_recv.at[source], device_id=partner, device_id_type=MESH,
        ).wait_recv()

    near = [me, x * 2 + 1 - c]
    others = [lax.rem(x * 2 + i, n_seq) for i in range(2, n_seq)]
    wait_kv(near[1])
    for h in range(GROUP):
        top, total, numer = attend(h, near, None)
        tops[h], totals[h], numers[h] = top, total, numer
    for source in others:
        wait_kv(source)
    for h in range(GROUP):
        top, total, numer = attend(h, others, (tops[h], totals[h], numers[h]))
        out_ref[:, pl.ds(h * HEAD, HEAD)] = (numer / total).astype(jnp.bfloat16)

    for cond, copy in pending:
        if cond is None:
            copy.wait_send()
        else:
            pl.when(cond)(copy.wait_send)


def fused_shards(hidden, queries, kv_weight, dest_device, segment_ids):
    n_seq, n_dp = lax.axis_size("seq"), lax.axis_size("dp")
    ny, nx = 2, n_seq // 2
    nz = n_dp // ny
    rows, d_model = hidden.shape
    depth, width = kv_weight.shape
    blocks = n_dp * n_seq
    width_q = queries.shape[1]
    keys = n_seq * rows
    dma = pltpu.SemaphoreType.DMA
    anyspace = pl.BlockSpec(memory_space=pl.ANY)
    vmem = pl.BlockSpec(memory_space=pltpu.VMEM)
    bf16, f32 = jnp.bfloat16, jnp.float32
    return pl.pallas_call(
        functools.partial(fused, nz, ny, nx),
        out_shape=jax.ShapeDtypeStruct((rows, width_q), bf16),
        in_specs=[anyspace, anyspace, anyspace, vmem, vmem],
        out_specs=vmem,
        scratch_shapes=[
            pltpu.VMEM((rows, d_model), bf16),
            pltpu.VMEM((rows, width_q), bf16),
            pltpu.VMEM((blocks, depth, width), bf16),
            pltpu.VMEM((n_seq, rows // 4, width_q), bf16),
            pltpu.VMEM((n_seq, rows // 4, width_q), bf16),
            pltpu.VMEM((n_seq, 1, rows), jnp.int32),
            pltpu.VMEM((n_seq, rows, width), bf16),
            pltpu.VMEM((rows, width_q), bf16),
            pltpu.VMEM((rows, keys), f32),
            pltpu.VMEM((rows, width), f32),
            pltpu.VMEM((GROUP, rows, 1), f32),
            pltpu.VMEM((GROUP, rows, 1), f32),
            pltpu.VMEM((GROUP, rows, HEAD), f32),
            dma((3,)),
            dma((PIECES * (9 + 9 * nz),)),
            dma((blocks, PIECES)),
            dma((3 * n_seq,)),
            dma((n_seq,)),
            dma((n_seq,)),
            dma((n_seq,)),
        ],
        compiler_params=pltpu.CompilerParams(
            collective_id=0, has_side_effects=True, vmem_limit_bytes=32 * 1024 * 1024
        ),
    )(hidden, queries, kv_weight, dest_device.reshape(1, rows), segment_ids)


def solution(mesh):
    in_specs = (
        P(("dp", "seq"), None),
        P(("dp", "seq"), None),
        P(("dp", "seq"), None),
        P(("dp", "seq")),
        P("dp", None),
    )
    out_specs = P(("dp", "seq"), None)
    n_dp, n_seq = mesh.shape["dp"], mesh.shape["seq"]
    body = fused_shards if n_seq == 4 and n_dp % 2 == 0 and 4 <= n_dp <= 16 else shards
    return jax.shard_map(body, mesh=mesh, in_specs=in_specs, out_specs=out_specs, check_vma=False)
```
